256 devices in a mesh: space: 128 (over x, y, z), chan: 2 (over core).
Axes of the slice: x: 4, y: 4, z: 8, core: 2. Of those that a mesh axis runs over, the one named last changes fastest.
Arguments:
- features: bfloat16 [262144, 256], P('space', 'chan'), may hold values from -6 to 6
- weights: bfloat16 [27, 256, 256], replicated, may hold values from -0.078125 to 0.078125
- cotangent: bfloat16 [262144, 256], P('space', 'chan'), may hold values from -6 to 6
- pair_offset: int32 [24576], P('space'), may hold values from 0 to 26
- pair_block: int32 [24576], P('space'), may hold values from 0 to 15
- pair_rows: int32 [24576, 128], P('space'), may hold values from 0 to 127
- pair_mask: int32 [24576, 128], P('space'), may hold values 0 or 1
- pair_dest_block: int32 [24576], P('space'), may hold values from 0 to 15
- remote_dest: int32 [16384, 1], P('space'), may hold values from 0 to 127; in each aligned block of 128 rows (0 to 127, 128 to 255, ...) at most 2 rows name the same one
Outputs:
- output: bfloat16 [262144, 256], P('space', 'chan')
- input_grad: bfloat16 [262144, 256], P('space', 'chan')
- weight_grad: float32 [27, 256, 256], P(None, None, 'chan')
The draws below stay inside these ranges and needn't reach their ends.
Inputs may be any that keep to these rules, and one draw needn't show every extreme that they name: `remote_dest`: among the 128 remote entries of one index of space, no owner is named more than 2 times, and in some indices one owner is named exactly 2 times.
All inputs are finite; a program needn't handle non-finite values. No bound on the sum of `pair_mask` on one device may be relied on, other than what follows from the above.
Results may differ from the reference program's by a relative error of at most 0.009.
Values may be sent and summed in bfloat16 or wider, within the bound.
No kernel may reach another device: no remote copies, remote signals or barrier semaphores. Data moves between devices by JAX's collectives and lax.ppermute only.
A program may use at most 192 MiB of HBM per device.

```python
import math
import jax
import jax.numpy as jnp
import numpy as np
from jax import lax

C = 256
K = 27
BLK = 128
NBD = 16
LOCAL_DEV = 64
REMOTE_DEV = 128
CAP = 2
BLOCKS = 2048
VOXELS = 262144
PAIRS = 24576
REMOTE = 16384
N_SPACE = 128


def plant(result, stream_key, least, top_value):
    longest = result.shape.index(max(result.shape))
    spots = []
    for shift in (0, 1):
        where = [jax.random.randint(jax.random.fold_in(stream_key, axis), (), 0, length) for axis, length in enumerate(result.shape)]
        where[longest] = (where[longest] + shift) % result.shape[longest]
        spots.append(tuple(where))
    return result.at[spots[0]].set(least).at[spots[1]].set(top_value)


def block_levels(own_key, dims, split, smallest, top_value):
    gain, own = 1.0, jax.random.fold_in(own_key, 6)
    for axis_at, blocks in split:
        draws = jnp.exp(jax.random.uniform(jax.random.fold_in(own, axis_at), (blocks,), jnp.float32, smallest / len(split), top_value / len(split)))
        gain = gain * jnp.repeat(draws, dims[axis_at] // blocks).reshape([-1 if axis == axis_at else 1 for axis in range(len(dims))])
    return gain


def assign_block(stream_key, own, number, rows, number_of, top, reach, slope):
    order = jax.random.permutation(stream_key, number_of)
    crowded, common = shares(number_of, rows * top, reach, slope, True), shares(number_of, rows * top, reach, slope, False)
    places = jnp.arange(number_of)

    def named(tallies, turn):
        used = int((tallies > 0).sum())
        fixed = max(1, used // 4)
        passed = fixed + (places - fixed + turn * (used - fixed)) % max(1, number_of - fixed)
        return jnp.zeros((number_of,), jnp.int32).at[order[jnp.where(places < fixed, places, passed)]].set(jnp.asarray(tallies, jnp.int32))

    tallies = jnp.where(number % 4 == 0, named(crowded, number // 4), named(common, number - number // 4 - 1))
    mixed = jax.random.permutation(jax.random.fold_in(own, 3), number_of)
    giver, receiver = mixed[0:number_of // 2 * 2:2], mixed[1:number_of // 2 * 2:2]
    margin = jnp.minimum(tallies[giver] - 1, reach - tallies[receiver]) // 2
    margin = jnp.where((giver == order[0]) | (receiver == order[0]) | (tallies[receiver] == 0), 0, jnp.maximum(margin, 0))
    passed = jax.random.randint(jax.random.fold_in(own, 4), (number_of // 2,), 0, 1 << 20) % (margin + 1)
    tallies = tallies.at[giver].add(-passed).at[receiver].add(passed)
    labels = jnp.searchsorted(jnp.cumsum(tallies), jnp.arange(rows * top), side="right").astype(jnp.int32)
    listing = labels.reshape(top, rows).T
    listing = listing[jax.random.permutation(jax.random.fold_in(own, 1), rows)]
    turn = jax.random.randint(jax.random.fold_in(own, 2), (rows, 1), 0, top)
    return jnp.take_along_axis(listing, (jnp.arange(top)[None, :] + turn) % top, axis=1)


def shares(number_of, total, bound, slope, full):
    weights = [(1 << 20) // math.isqrt(rank ** slope) + 1 for rank in range(1, number_of + 1)]
    largest = bound if full else min(bound, max(-(-total // number_of), total * weights[0] // sum(weights)))
    least = 1 if total - largest >= number_of - 1 else 0
    holding, surplus = [largest] + [least] * (number_of - 1), total - largest - least * (number_of - 1)
    while surplus > 0:
        free = [i for i in range(1, number_of) if holding[i] < largest] or [i for i in range(1, number_of) if holding[i] < bound]
        mass, remaining = sum([weights[i] for i in free]), surplus
        for i in free:
            extra = min(bound - holding[i], max(1, remaining * weights[i] // mass), surplus)
            holding[i] = holding[i] + extra
            surplus = surplus - extra
    return np.array(holding)


def bell_draw(own_key, shape, width, limit, shards=(), kind=jnp.bfloat16):
    gain = block_levels(own_key, shape, shards, -0.22, 0.18) if shards else 1.0
    entries = jax.random.normal(own_key, shape, jnp.float32) * width * gain
    return jnp.minimum(jnp.maximum(entries, -limit), limit).astype(kind)


def setup_inputs(seed: int = 0) -> dict:
    seeds = jax.random.split(jax.random.key(seed), 10)
    features = bell_draw(seeds[0], (VOXELS, C), 1.0, 6.0, ((0, 128), (1, 2)))
    weights = bell_draw(seeds[1], (K, C, C), (K * C) ** -0.5, 0.078125)
    cotangent = bell_draw(seeds[2], (VOXELS, C), 1.0, 6.0, ((0, 128), (1, 2)))
    pair_offset = plant(jax.random.randint(seeds[3], (PAIRS,), 0, K), jax.random.fold_in(seeds[3], 1), 0, K - 1).astype(jnp.int32)
    pair_block = plant(jax.random.randint(seeds[4], (PAIRS,), 0, NBD), jax.random.fold_in(seeds[4], 1), 0, NBD - 1).astype(jnp.int32)
    pair_rows = plant(jax.random.randint(seeds[5], (PAIRS, BLK), 0, BLK), jax.random.fold_in(seeds[5], 1), 0, BLK - 1).astype(jnp.int32)
    pair_mask = plant((jax.random.randint(seeds[6], (PAIRS, BLK), 0, 4) < 3).astype(jnp.int32), jax.random.fold_in(seeds[6], 1), 0, 1)
    pair_dest_block = plant(jax.random.randint(seeds[7], (PAIRS,), 0, NBD), jax.random.fold_in(seeds[7], 1), 0, NBD - 1).astype(jnp.int32)
    remote_dest_keys = jax.random.split(jax.random.fold_in(seeds[8], 1), REMOTE // REMOTE_DEV)
    remote_dest_turns = jax.random.permutation(jax.random.fold_in(seeds[8], 3), REMOTE // REMOTE_DEV)
    remote_dest = jax.vmap(lambda own, number: assign_block(jax.random.fold_in(seeds[8], 2), own, number, REMOTE_DEV, N_SPACE, 1, CAP, 2))(remote_dest_keys, remote_dest_turns).reshape((REMOTE, 1))
    return dict(features=features, weights=weights, cotangent=cotangent, pair_offset=pair_offset, pair_block=pair_block, pair_rows=pair_rows, pair_mask=pair_mask, pair_dest_block=pair_dest_block, remote_dest=remote_dest)


def reference(features, weights, cotangent, pair_offset, pair_block, pair_rows, pair_mask, pair_dest_block, remote_dest):
    per_device = LOCAL_DEV + REMOTE_DEV
    owner_ids = jnp.arange(N_SPACE, dtype=jnp.int32)
    dest_device = jnp.concatenate([jnp.broadcast_to(owner_ids[:, None], (N_SPACE, LOCAL_DEV)), remote_dest.reshape(N_SPACE, REMOTE_DEV)], axis=1).astype(jnp.int32)
    travels_flag = jnp.concatenate([jnp.zeros((N_SPACE, LOCAL_DEV), jnp.int32), jnp.ones((N_SPACE, REMOTE_DEV), jnp.int32)], axis=1)
    cot_blocks = cotangent.reshape(BLOCKS, BLK, C)

    def one_device(totals, inputs):
        out_sum, input_sum, weight_sum = totals
        owner_id, offsets, blocks, row_map, row_mask, dest_block, dest_dev, moved_flag = inputs
        source = owner_id * (NBD * BLK) + blocks[:, None] * BLK + row_map
        alive = row_mask.astype(jnp.float32)[:, :, None]
        gathered = features[source].astype(jnp.float32) * alive
        kernel = weights[offsets].astype(jnp.float32)
        partial_value = jnp.einsum("pri,pio->pro", gathered, kernel)
        rounded = lax.optimization_barrier(partial_value.astype(jnp.bfloat16)).astype(jnp.float32)
        partial_value = jnp.where(moved_flag[:, None, None] == 1, rounded, partial_value)
        target = dest_dev * NBD + dest_block
        out_sum = out_sum.at[target].add(partial_value)
        upstream = cot_blocks[target].astype(jnp.float32)
        back_term = jnp.einsum("pro,pio->pri", upstream, kernel) * alive
        input_sum = input_sum.at[source.reshape(-1)].add(back_term.reshape(-1, C))
        outer_term = jnp.einsum("pri,pro->pio", gathered, upstream)
        weight_sum = weight_sum.at[offsets].add(outer_term)
        return (out_sum, input_sum, weight_sum), None

    initial = (jnp.zeros((BLOCKS, BLK, C), jnp.float32), jnp.zeros((VOXELS, C), jnp.float32), jnp.zeros((K, C, C), jnp.float32))
    per_inputs = (owner_ids, pair_offset.reshape(N_SPACE, per_device), pair_block.reshape(N_SPACE, per_device), pair_rows.reshape(N_SPACE, per_device, BLK), pair_mask.reshape(N_SPACE, per_device, BLK), pair_dest_block.reshape(N_SPACE, per_device), dest_device, travels_flag)
    (out_sum, input_sum, weight_sum), _ = lax.scan(one_device, initial, per_inputs)
    grad_scale = (K / (PAIRS * BLK)) ** 0.5
    return (out_sum.reshape(VOXELS, C).astype(jnp.bfloat16), input_sum.astype(jnp.bfloat16), weight_sum * grad_scale)
```

```python
import jax
import jax.numpy as jnp
from jax import lax
from jax.experimental import pallas as pl
from jax.experimental.pallas import tpu as pltpu
from jax.sharding import Mesh
from jax.sharding import PartitionSpec as P

SPACE = ("x", "y", "z")
PLANE = ("x", "y")
FACTORS = {128: (4, 4, 8), 8: (2, 2, 2)}
BF16 = jnp.bfloat16
F32 = jnp.float32

VM = pl.BlockSpec(memory_space=pltpu.VMEM)
SM = pl.BlockSpec(memory_space=pltpu.SMEM)


def pick_transposed(rows_ref, at, block_rows):
    rows = rows_ref[pl.ds(at, 1), :]
    lines = lax.broadcasted_iota(jnp.int32, (block_rows, rows.shape[1]), 0)
    return jnp.where(lines == rows, 1.0, 0.0).astype(BF16)


def forward_block(picked, feats, kernel):
    rows = lax.dot_general(
        picked, feats, (((0,), (0,)), ((), ())), preferred_element_type=F32
    ).astype(BF16)
    return jnp.dot(rows, kernel, preferred_element_type=F32)


def backward_block(picked, upstream, feats_t, kernel, in_ref, block, w_ref, offset):
    spread = jnp.dot(picked, upstream, preferred_element_type=F32).astype(BF16)
    in_ref[block] += lax.dot_general(
        spread, kernel, (((1,), (1,)), ((), ())), preferred_element_type=F32
    )
    w_ref[offset] += jnp.dot(feats_t, spread, preferred_element_type=F32)


def send_kernel(offset, block, slot, rows_ref, feat_ref, kern_ref, first_ref, last_ref):
    half = first_ref.shape[1]

    def step(q, carry):
        picked = pick_transposed(rows_ref, q, feat_ref.shape[1])
        part = forward_block(picked, feat_ref[block[q]], kern_ref[offset[q]]).astype(BF16)
        first_ref[slot[q]] = part[:half]
        last_ref[slot[q]] = part[half:]
        return carry

    lax.fori_loop(0, rows_ref.shape[0], step, 0, unroll=4)


def pack_kernel(code, cot_ref, out_ref):
    def step(s, carry):
        out_ref[s] = cot_ref[code[s]]
        return carry

    lax.fori_loop(0, out_ref.shape[0], step, 0, unroll=8)


def local_kernel(
    offset, block, dest, rows_ref, feat_ref, feat_t_ref, kern_ref, cot_ref, res_ref, in_ref, w_ref
):
    res_ref[...] = jnp.zeros_like(res_ref)
    in_ref[...] = jnp.zeros_like(in_ref)
    w_ref[...] = jnp.zeros_like(w_ref)

    def step(q, carry):
        b, k, d = block[q], offset[q], dest[q]
        picked = pick_transposed(rows_ref, q, feat_ref.shape[1])
        kernel = kern_ref[k]
        res_ref[d] += forward_block(picked, feat_ref[b], kernel)
        backward_block(picked, cot_ref[d], feat_t_ref[b], kernel, in_ref, b, w_ref, k)
        return carry

    lax.fori_loop(0, rows_ref.shape[0], step, 0, unroll=2)


def remote_kernel(
    offset, block, slot, rows_ref, feat_t_ref, kern_ref, up_ref, in0_ref, w0_ref, in_ref, w_ref
):
    in_ref[...] = in0_ref[...]
    w_ref[...] = w0_ref[...]

    def step(q, carry):
        b, k = block[q], offset[q]
        picked = pick_transposed(rows_ref, q, feat_t_ref.shape[2])
        backward_block(
            picked, up_ref[slot[q]], feat_t_ref[b], kern_ref[k], in_ref, b, w_ref, k
        )
        return carry

    lax.fori_loop(0, rows_ref.shape[0], step, 0, unroll=4)


def column_kernel(code, recv_ref, out_ref, acc_ref):
    acc_ref[...] = jnp.zeros_like(acc_ref)

    def step(s, carry):
        acc_ref[code[s]] += recv_ref[s].astype(F32)
        return carry

    lax.fori_loop(0, recv_ref.shape[0], step, 0, unroll=4)

    def put(b, carry):
        out_ref[b] = acc_ref[b].astype(BF16)
        return carry

    lax.fori_loop(0, out_ref.shape[0], put, 0, unroll=8)


def call(kernel, scalars, arrays, outs, scratch=(), flops=0):
    moved = sum(a.size * a.dtype.itemsize for a in arrays)
    moved += sum(o.size * o.dtype.itemsize for o in outs)
    return pl.pallas_call(
        kernel,
        out_shape=outs,
        in_specs=[SM] * len(scalars) + [VM] * len(arrays),
        out_specs=[VM] * len(outs),
        scratch_shapes=list(scratch),
        cost_estimate=pl.CostEstimate(flops=flops, bytes_accessed=moved, transcendentals=0),
    )(*scalars, *arrays)


def after(a, *others):
    return lax.optimization_barrier((a,) + others)[0]


def plane_exchange(a):
    return lax.all_to_all(a, PLANE, split_axis=0, concat_axis=0, tiled=True)


def reduce_weights(total, kernels, in_width, out_width, ahead, last):
    columns = lax.axis_size("z")
    planes = lax.axis_size("x") * lax.axis_size("y")
    flat = total.reshape(kernels * in_width, out_width).astype(BF16)
    part = after(lax.psum_scatter(flat, "z", scatter_dimension=0, tiled=True), ahead)
    rows = part.shape[0]
    each = -(-rows // (planes * 16)) * 16
    part = jnp.pad(part, ((0, planes * each - rows), (0, 0)))
    pieces = plane_exchange(part).reshape(planes, each, out_width)
    summed = jnp.sum(pieces.astype(F32), axis=0).astype(BF16)
    spread = jnp.broadcast_to(summed[None], (planes, each, out_width))
    whole = plane_exchange(spread.reshape(planes * each, out_width))[:rows]
    return lax.all_gather(after(whole, last), "z", axis=0, tiled=True).astype(F32)


def body(
    features,
    weights,
    cotangent,
    pair_offset,
    pair_block,
    pair_rows,
    pair_mask,
    pair_dest_block,
    remote_dest,
):
    columns = lax.axis_size("z")
    planes = lax.axis_size("x") * lax.axis_size("y")
    chan = lax.axis_index("chan")
    row_count, width = features.shape
    kernels, in_width, _ = weights.shape
    pair_count, rows = pair_rows.shape
    remote = remote_dest.shape[0]
    local = pair_count - remote
    blocks = row_count // rows
    depth = 2 * columns
    slots = planes * depth
    half = rows // 2

    dest = remote_dest[:, 0]
    plane_of = dest // columns
    wanted = (dest % columns) * blocks + pair_dest_block[local:]
    order = jnp.arange(remote, dtype=jnp.int32)
    same = (plane_of[:, None] == plane_of[None, :]) & (order[None, :] < order[:, None])
    slot = plane_of * depth + jnp.sum(same.astype(jnp.int32), axis=1)
    hits = slot[None, :] == jnp.arange(slots, dtype=jnp.int32)[:, None]
    sent_code = jnp.max(jnp.where(hits, wanted[None, :], -1), axis=1)
    code = plane_exchange(sent_code)

    picks = jnp.where(pair_mask > 0, pair_rows, rows)
    kern = lax.dynamic_slice_in_dim(weights, chan * width, width, 2)
    other = lax.ppermute(features, "chan", [(0, 1), (1, 0)])
    low = jnp.where(chan == 0, features, other)
    high = jnp.where(chan == 0, other, features)
    feats = jnp.concatenate([low, high], axis=1).reshape(blocks, rows, in_width)

    sent = call(
        send_kernel,
        (pair_offset[local:], pair_block[local:], slot),
        (picks[local:], feats, kern),
        [
            jax.ShapeDtypeStruct((slots, half, width), BF16),
            jax.ShapeDtypeStruct((slots, rows - half, width), BF16),
        ],
        flops=2 * remote * rows * in_width * (rows + width),
    )
    came_first = plane_exchange(after(sent[0], code))
    column_cot = lax.all_gather(cotangent, "z", axis=0, tiled=True)

    feats_t = jnp.swapaxes(feats, 1, 2)
    resident, in_sum, w_sum = call(
        local_kernel,
        (pair_offset[:local], pair_block[:local], pair_dest_block[:local]),
        (after(picks[:local], sent[0]), feats, feats_t, kern, cotangent.reshape(blocks, rows, width)),
        [
            jax.ShapeDtypeStruct((blocks, rows, width), F32),
            jax.ShapeDtypeStruct((blocks, rows, in_width), F32),
            jax.ShapeDtypeStruct((kernels, in_width, width), F32),
        ],
        flops=2 * local * rows * in_width * (rows + width) * 2,
    )

    valid_code = jnp.maximum(code, 0)
    sum_code = jnp.where(code < 0, columns * blocks, code)
    packed = call(
        pack_kernel,
        (after(valid_code, resident),),
        (column_cot.reshape(columns * blocks, rows, width),),
        [jax.ShapeDtypeStruct((slots, rows, width), BF16)],
    )[0]
    upstream = plane_exchange(after(packed, came_first))

    def column_total(came):
        return call(
            column_kernel,
            (sum_code,),
            (came,),
            [jax.ShapeDtypeStruct((columns * blocks,) + came.shape[1:], BF16)],
            [pltpu.VMEM((columns * blocks + 1,) + came.shape[1:], F32)],
        )[0]

    first_total = column_total(came_first)
    first_sum = lax.psum_scatter(first_total, "z", scatter_dimension=0, tiled=True)
    came_last = plane_exchange(after(sent[1], upstream, first_total))

    in_sum, w_sum = call(
        remote_kernel,
        (pair_offset[local:], pair_block[local:], slot),
        (picks[local:], feats_t, kern, after(upstream, first_sum), in_sum, w_sum),
        [
            jax.ShapeDtypeStruct((blocks, rows, in_width), F32),
            jax.ShapeDtypeStruct((kernels, in_width, width), F32),
        ],
        flops=2 * remote * rows * in_width * (rows + width),
    )
    last_total = column_total(came_last)
    last_sum = lax.psum_scatter(last_total, "z", scatter_dimension=0, tiled=True)

    grad_scale = (kernels / (pair_count * columns * planes * rows)) ** 0.5
    weight_grad = reduce_weights(w_sum, kernels, in_width, width, last_total, last_sum) * grad_scale
    weight_grad = weight_grad.reshape(kernels, in_width, width)

    in_sum = in_sum.reshape(row_count, in_width)
    mine = lax.dynamic_slice_in_dim(in_sum, chan * width, width, 1)
    theirs = lax.dynamic_slice_in_dim(in_sum, (1 - chan) * width, width, 1)
    theirs = lax.ppermute(theirs.astype(BF16), "chan", [(0, 1), (1, 0)])
    input_grad = (mine + theirs.astype(F32)).astype(BF16)

    output = resident + jnp.concatenate([first_sum, last_sum], axis=1).astype(F32)
    output = output.reshape(row_count, width).astype(BF16)
    return (output, input_grad, weight_grad)


def solution(mesh):
    x, y, z = FACTORS[mesh.devices.shape[0]]
    split = Mesh(mesh.devices.reshape(x, y, z, -1), SPACE + ("chan",))
    in_specs = (
        P(SPACE, "chan"),
        P(),
        P(SPACE, "chan"),
        P(SPACE),
        P(SPACE),
        P(SPACE, None),
        P(SPACE, None),
        P(SPACE),
        P(SPACE, None),
    )
    out_specs = (P(SPACE, "chan"), P(SPACE, "chan"), P(None, None, "chan"))
    return jax.shard_map(body, mesh=split, in_specs=in_specs, out_specs=out_specs, check_vma=False)
```

```python
import jax
import jax.numpy as jnp
from jax import lax
from jax.experimental import pallas as pl
from jax.experimental.pallas import tpu as pltpu
from jax.sharding import Mesh
from jax.sharding import PartitionSpec as P

SPACE = ("x", "y", "z")
PLANE = ("x", "y")
FACTORS = {128: (4, 4, 8), 8: (2, 2, 2)}
BF16 = jnp.bfloat16
F32 = jnp.float32

VM = pl.BlockSpec(memory_space=pltpu.VMEM)
SM = pl.BlockSpec(memory_space=pltpu.SMEM)


def pick_transposed(rows_ref, at, block_rows):
    rows = rows_ref[pl.ds(at, 1), :]
    lines = lax.broadcasted_iota(jnp.int32, (block_rows, rows.shape[1]), 0)
    return jnp.where(lines == rows, 1.0, 0.0).astype(BF16)


def forward_block(picked, feats, kernel):
    rows = lax.dot_general(
        picked, feats, (((0,), (0,)), ((), ())), preferred_element_type=F32
    ).astype(BF16)
    return jnp.dot(rows, kernel, preferred_element_type=F32)


def backward_block(picked, upstream, feats_t, kernel, in_ref, block, w_ref, offset):
    spread = jnp.dot(picked, upstream, preferred_element_type=F32).astype(BF16)
    in_ref[block] += lax.dot_general(
        spread, kernel, (((1,), (1,)), ((), ())), preferred_element_type=F32
    )
    w_ref[offset] += jnp.dot(feats_t, spread, preferred_element_type=F32)


def send_kernel(offset, block, rows_ref, feat_ref, kern_ref, out_ref):
    def step(q, carry):
        picked = pick_transposed(rows_ref, q, feat_ref.shape[1])
        out_ref[q] = forward_block(picked, feat_ref[block[q]], kern_ref[offset[q]]).astype(BF16)
        return carry

    lax.fori_loop(0, rows_ref.shape[0], step, 0, unroll=4)


def place_kernel(slot, part_ref, out_ref):
    def step(q, carry):
        out_ref[slot[q]] = part_ref[q]
        return carry

    lax.fori_loop(0, part_ref.shape[0], step, 0, unroll=8)


def pack_kernel(code, cot_ref, out_ref):
    def step(s, carry):
        out_ref[s] = cot_ref[code[s]]
        return carry

    lax.fori_loop(0, out_ref.shape[0], step, 0, unroll=8)


def local_kernel(
    offset, block, dest, rows_ref, feat_ref, feat_t_ref, kern_ref, cot_ref, res_ref, in_ref, w_ref
):
    res_ref[...] = jnp.zeros_like(res_ref)
    in_ref[...] = jnp.zeros_like(in_ref)
    w_ref[...] = jnp.zeros_like(w_ref)

    def step(q, carry):
        b, k, d = block[q], offset[q], dest[q]
        picked = pick_transposed(rows_ref, q, feat_ref.shape[1])
        kernel = kern_ref[k]
        res_ref[d] += forward_block(picked, feat_ref[b], kernel)
        backward_block(picked, cot_ref[d], feat_t_ref[b], kernel, in_ref, b, w_ref, k)
        return carry

    lax.fori_loop(0, rows_ref.shape[0], step, 0, unroll=2)


def remote_kernel(
    offset, block, slot, rows_ref, feat_t_ref, kern_ref, up_ref, in0_ref, w0_ref, in_ref, w_ref
):
    in_ref[...] = in0_ref[...]
    w_ref[...] = w0_ref[...]

    def step(q, carry):
        b, k = block[q], offset[q]
        picked = pick_transposed(rows_ref, q, feat_t_ref.shape[2])
        backward_block(
            picked, up_ref[slot[q]], feat_t_ref[b], kern_ref[k], in_ref, b, w_ref, k
        )
        return carry

    lax.fori_loop(0, rows_ref.shape[0], step, 0, unroll=4)


def column_kernel(code, recv_ref, out_ref, acc_ref):
    acc_ref[...] = jnp.zeros_like(acc_ref)

    def step(s, carry):
        acc_ref[code[s]] += recv_ref[s].astype(F32)
        return carry

    lax.fori_loop(0, recv_ref.shape[0], step, 0, unroll=4)

    def put(b, carry):
        out_ref[b] = acc_ref[b].astype(BF16)
        return carry

    lax.fori_loop(0, out_ref.shape[0], put, 0, unroll=8)


def call(kernel, scalars, arrays, outs, scratch=(), flops=0):
    moved = sum(a.size * a.dtype.itemsize for a in arrays)
    moved += sum(o.size * o.dtype.itemsize for o in outs)
    return pl.pallas_call(
        kernel,
        out_shape=outs,
        in_specs=[SM] * len(scalars) + [VM] * len(arrays),
        out_specs=[VM] * len(outs),
        scratch_shapes=list(scratch),
        cost_estimate=pl.CostEstimate(flops=flops, bytes_accessed=moved, transcendentals=0),
    )(*scalars, *arrays)


def after(a, *others):
    return lax.optimization_barrier((a,) + others)[0]


def plane_exchange(a):
    return lax.all_to_all(a, PLANE, split_axis=0, concat_axis=0, tiled=True)


def spread_weights(pieces, planes):
    summed = jnp.sum(pieces.astype(F32), axis=0).astype(BF16)
    columns = lax.all_gather(summed, "z", axis=0, tiled=False)
    whole = jnp.sum(columns.astype(F32), axis=0).astype(BF16)
    copies = jnp.broadcast_to(whole[None], (planes,) + whole.shape)
    return plane_exchange(copies.reshape(-1, whole.shape[1]))


def body(
    features,
    weights,
    cotangent,
    pair_offset,
    pair_block,
    pair_rows,
    pair_mask,
    pair_dest_block,
    remote_dest,
):
    columns = lax.axis_size("z")
    planes = lax.axis_size("x") * lax.axis_size("y")
    chan = lax.axis_index("chan")
    row_count, width = features.shape
    kernels, in_width, _ = weights.shape
    pair_count, rows = pair_rows.shape
    remote = remote_dest.shape[0]
    local = pair_count - remote
    blocks = row_count // rows
    depth = 2 * columns
    shallow = depth * 3 // 4

    column_cot = lax.all_gather(cotangent, "z", axis=0, tiled=True)
    column_cot = column_cot.reshape(columns * blocks, rows, width)

    dest = remote_dest[:, 0]
    plane_of = dest // columns
    wanted = (dest % columns) * blocks + pair_dest_block[local:]
    order = jnp.arange(remote, dtype=jnp.int32)
    same = (plane_of[:, None] == plane_of[None, :]) & (order[None, :] < order[:, None])
    rank = jnp.sum(same.astype(jnp.int32), axis=1)
    slot = plane_of * depth + rank
    hits = slot[None, :] == jnp.arange(planes * depth, dtype=jnp.int32)[:, None]
    sent_code = jnp.max(jnp.where(hits, wanted[None, :], -1), axis=1)
    code = plane_exchange(sent_code)
    most = jnp.broadcast_to(jnp.max(rank), (planes * columns,))
    most = lax.all_to_all(after(most, code), SPACE, split_axis=0, concat_axis=0, tiled=True)
    fits = jnp.max(most) < shallow

    picks = jnp.where(pair_mask > 0, pair_rows, rows)
    kern = lax.dynamic_slice_in_dim(weights, chan * width, width, 2)
    other = lax.ppermute(features, "chan", [(0, 1), (1, 0)])
    low = jnp.where(chan == 0, features, other)
    high = jnp.where(chan == 0, other, features)
    feats = jnp.concatenate([low, high], axis=1).reshape(blocks, rows, in_width)
    feats_t = jnp.swapaxes(feats, 1, 2)
    cot_blocks = cotangent.reshape(blocks, rows, width)
    sums = [
        jax.ShapeDtypeStruct((blocks, rows, in_width), F32),
        jax.ShapeDtypeStruct((kernels, in_width, width), F32),
    ]

    parts = call(
        send_kernel,
        (pair_offset[local:], pair_block[local:]),
        (picks[local:], feats, kern),
        [jax.ShapeDtypeStruct((remote, rows, width), BF16)],
        flops=2 * remote * rows * in_width * (rows + width),
    )[0]

    def exchange(deep):
        slots = planes * deep
        place = plane_of * deep + rank
        codes = code.reshape(planes, depth)[:, :deep].reshape(slots)
        boxes = [jax.ShapeDtypeStruct((slots, rows, width), BF16)]

        packed = call(pack_kernel, (jnp.maximum(codes, 0),), (column_cot,), boxes)[0]
        upstream = plane_exchange(packed)

        resident, in_sum, w_sum = call(
            local_kernel,
            (pair_offset[:local], pair_block[:local], pair_dest_block[:local]),
            (after(picks[:local], packed), feats, feats_t, kern, cot_blocks),
            [jax.ShapeDtypeStruct((blocks, rows, width), F32)] + sums,
            flops=4 * local * rows * in_width * (rows + width),
        )
        placed = call(place_kernel, (place,), (after(parts, packed),), boxes)[0]
        came = plane_exchange(after(placed, upstream, resident))

        in_sum, w_sum = call(
            remote_kernel,
            (pair_offset[local:], pair_block[local:], place),
            (picks[local:], feats_t, kern, upstream, in_sum, w_sum),
            sums,
            flops=2 * remote * rows * in_width * (rows + width),
        )
        flat = w_sum.reshape(kernels * in_width, width).astype(BF16)
        pieces = plane_exchange(after(flat, came))
        column_sum = call(
            column_kernel,
            (jnp.where(codes < 0, columns * blocks, codes),),
            (came,),
            [jax.ShapeDtypeStruct((columns * blocks, rows, width), BF16)],
            [pltpu.VMEM((columns * blocks + 1, rows, width), F32)],
        )[0]
        return resident, in_sum, pieces, column_sum

    resident, in_sum, pieces, column_sum = lax.cond(
        fits, lambda: exchange(shallow), lambda: exchange(depth)
    )

    arrived = lax.psum_scatter(column_sum, "z", scatter_dimension=0, tiled=True)
    output = (resident + arrived.astype(F32)).reshape(row_count, width).astype(BF16)

    grad_scale = (kernels / (pair_count * columns * planes * rows)) ** 0.5
    whole = spread_weights(pieces.reshape(planes, -1, width), planes)
    weight_grad = (whole.astype(F32) * grad_scale).reshape(kernels, in_width, width)

    in_sum = in_sum.reshape(row_count, in_width)
    mine = lax.dynamic_slice_in_dim(in_sum, chan * width, width, 1)
    theirs = lax.dynamic_slice_in_dim(in_sum, (1 - chan) * width, width, 1)
    theirs = lax.ppermute(theirs.astype(BF16), "chan", [(0, 1), (1, 0)])
    input_grad = (mine + theirs.astype(F32)).astype(BF16)
    return (output, input_grad, weight_grad)


def solution(mesh):
    x, y, z = FACTORS[mesh.devices.shape[0]]
    split = Mesh(mesh.devices.reshape(x, y, z, -1), SPACE + ("chan",))
    in_specs = (
        P(SPACE, "chan"),
        P(),
        P(SPACE, "chan"),
        P(SPACE),
        P(SPACE),
        P(SPACE, None),
        P(SPACE, None),
        P(SPACE),
        P(SPACE, None),
    )
    out_specs = (P(SPACE, "chan"), P(SPACE, "chan"), P(None, None, "chan"))
    return jax.shard_map(body, mesh=split, in_specs=in_specs, out_specs=out_specs, check_vma=False)
```

```python
import functools

import jax
import jax.numpy as jnp
from jax import lax
from jax.experimental import pallas as pl
from jax.experimental.pallas import tpu as pltpu
from jax.sharding import Mesh
from jax.sharding import PartitionSpec as P

SPACE = ("x", "y", "z")
PLANE = ("x", "y")
SHARES = (10, 11, 12, 16)
FACTORS = {128: (4, 4, 8), 8: (2, 2, 2)}
BF16 = jnp.bfloat16
F32 = jnp.float32

VM = pl.BlockSpec(memory_space=pltpu.VMEM)
SM = pl.BlockSpec(memory_space=pltpu.SMEM)


def pick_transposed(rows_ref, at, block_rows):
    rows = rows_ref[pl.ds(at, 1), :]
    lines = lax.broadcasted_iota(jnp.int32, (block_rows, rows.shape[1]), 0)
    return jnp.where(lines == rows, 1.0, 0.0).astype(BF16)


def forward_block(picked, feats, kernel):
    rows = lax.dot_general(
        picked, feats, (((0,), (0,)), ((), ())), preferred_element_type=F32
    ).astype(BF16)
    return jnp.dot(rows, kernel, preferred_element_type=F32)


def backward_block(picked, upstream, feats_t, kernel, in_ref, block, w_ref, offset):
    spread = jnp.dot(picked, upstream, preferred_element_type=F32).astype(BF16)
    in_ref[block] += lax.dot_general(
        spread, kernel, (((1,), (1,)), ((), ())), preferred_element_type=F32
    )
    w_ref[offset] += jnp.dot(feats_t, spread, preferred_element_type=F32)


def send_kernel(offset, block, rows_ref, feat_ref, kern_ref, out_ref):
    def step(q, carry):
        picked = pick_transposed(rows_ref, q, feat_ref.shape[1])
        out_ref[q] = forward_block(picked, feat_ref[block[q]], kern_ref[offset[q]]).astype(BF16)
        return carry

    lax.fori_loop(0, rows_ref.shape[0], step, 0, unroll=4)


def place_kernel(slot, part_ref, out_ref):
    def step(q, carry):
        out_ref[slot[q]] = part_ref[q]
        return carry

    lax.fori_loop(0, part_ref.shape[0], step, 0, unroll=8)


def pack_kernel(code, cot_ref, out_ref):
    def step(s, carry):
        out_ref[s] = cot_ref[code[s]]
        return carry

    lax.fori_loop(0, out_ref.shape[0], step, 0, unroll=8)


def local_kernel(
    offset, block, dest, rows_ref, feat_ref, feat_t_ref, kern_ref, cot_ref, res_ref, in_ref, w_ref
):
    res_ref[...] = jnp.zeros_like(res_ref)
    in_ref[...] = jnp.zeros_like(in_ref)
    w_ref[...] = jnp.zeros_like(w_ref)

    def step(q, carry):
        b, k, d = block[q], offset[q], dest[q]
        picked = pick_transposed(rows_ref, q, feat_ref.shape[1])
        kernel = kern_ref[k]
        res_ref[d] += forward_block(picked, feat_ref[b], kernel)
        backward_block(picked, cot_ref[d], feat_t_ref[b], kernel, in_ref, b, w_ref, k)
        return carry

    lax.fori_loop(0, rows_ref.shape[0], step, 0)


def remote_kernel(
    offset, block, slot, rows_ref, feat_t_ref, kern_ref, up_ref, in0_ref, w0_ref, in_ref, w_ref
):
    in_ref[...] = in0_ref[...]
    w_ref[...] = w0_ref[...]

    def step(q, carry):
        b, k = block[q], offset[q]
        picked = pick_transposed(rows_ref, q, feat_t_ref.shape[2])
        backward_block(
            picked, up_ref[slot[q]], feat_t_ref[b], kern_ref[k], in_ref, b, w_ref, k
        )
        return carry

    lax.fori_loop(0, rows_ref.shape[0], step, 0, unroll=2)


def column_kernel(code, recv_ref, out_ref, acc_ref):
    acc_ref[...] = jnp.zeros_like(acc_ref)

    def step(s, carry):
        acc_ref[code[s]] += recv_ref[s].astype(F32)
        return carry

    lax.fori_loop(0, recv_ref.shape[0], step, 0, unroll=4)

    def put(b, carry):
        out_ref[b] = acc_ref[b].astype(BF16)
        return carry

    lax.fori_loop(0, out_ref.shape[0], put, 0, unroll=8)


def call(kernel, scalars, arrays, outs, scratch=(), flops=0):
    moved = sum(a.size * a.dtype.itemsize for a in arrays)
    moved += sum(o.size * o.dtype.itemsize for o in outs)
    return pl.pallas_call(
        kernel,
        out_shape=outs,
        in_specs=[SM] * len(scalars) + [VM] * len(arrays),
        out_specs=[VM] * len(outs),
        scratch_shapes=list(scratch),
        cost_estimate=pl.CostEstimate(flops=flops, bytes_accessed=moved, transcendentals=0),
    )(*scalars, *arrays)


def after(a, *others):
    return lax.optimization_barrier((a,) + others)[0]


def axis_exchange(a, axes):
    return lax.all_to_all(a, axes, split_axis=0, concat_axis=0, tiled=True)


def spread(part, axes, count):
    copies = jnp.broadcast_to(part[None], (count,) + part.shape)
    return axis_exchange(copies.reshape((-1,) + part.shape[1:]), axes)


def summed(pieces, count):
    pieces = pieces.reshape((count, -1, pieces.shape[-1]))
    return jnp.sum(pieces.astype(F32), axis=0).astype(BF16)


def spread_weights(pieces, planes, columns):
    part = summed(pieces, planes)
    rows = part.shape[0]
    each = -(-rows // (columns * 16)) * 16
    part = jnp.pad(part, ((0, columns * each - rows), (0, 0)))
    part = summed(axis_exchange(part, "z"), columns)
    return spread(spread(part, "z", columns)[:rows], PLANE, planes)


def body(
    features,
    weights,
    cotangent,
    pair_offset,
    pair_block,
    pair_rows,
    pair_mask,
    pair_dest_block,
    remote_dest,
):
    columns = lax.axis_size("z")
    planes = lax.axis_size("x") * lax.axis_size("y")
    chan = lax.axis_index("chan")
    row_count, width = features.shape
    kernels, in_width, _ = weights.shape
    pair_count, rows = pair_rows.shape
    remote = remote_dest.shape[0]
    local = pair_count - remote
    blocks = row_count // rows
    depth = 2 * columns
    depths = sorted({depth * share // 16 for share in SHARES})

    column_cot = lax.all_gather(cotangent, "z", axis=0, tiled=True)
    column_cot = column_cot.reshape(columns * blocks, rows, width)

    dest = remote_dest[:, 0]
    plane_of = dest // columns
    wanted = (dest % columns) * blocks + pair_dest_block[local:]
    order = jnp.arange(remote, dtype=jnp.int32)
    same = (plane_of[:, None] == plane_of[None, :]) & (order[None, :] < order[:, None])
    rank = jnp.sum(same.astype(jnp.int32), axis=1)
    slot = plane_of * depth + rank
    hits = slot[None, :] == jnp.arange(planes * depth, dtype=jnp.int32)[:, None]
    sent_code = jnp.max(jnp.where(hits, wanted[None, :], -1), axis=1)
    code = axis_exchange(sent_code, PLANE)
    most = spread(after(jnp.max(rank, keepdims=True), code), SPACE, planes * columns)
    tier = jnp.sum((jnp.max(most) >= jnp.array(depths[:-1])).astype(jnp.int32))

    picks = jnp.where(pair_mask > 0, pair_rows, rows)
    kern = lax.dynamic_slice_in_dim(weights, chan * width, width, 2)
    other = lax.ppermute(features, "chan", [(0, 1), (1, 0)])
    low = jnp.where(chan == 0, features, other)
    high = jnp.where(chan == 0, other, features)
    feats = jnp.concatenate([low, high], axis=1).reshape(blocks, rows, in_width)
    feats_t = jnp.swapaxes(feats, 1, 2)
    cot_blocks = cotangent.reshape(blocks, rows, width)
    sums = [
        jax.ShapeDtypeStruct((blocks, rows, in_width), F32),
        jax.ShapeDtypeStruct((kernels, in_width, width), F32),
    ]

    parts = call(
        send_kernel,
        (pair_offset[local:], pair_block[local:]),
        (picks[local:], feats, kern),
        [jax.ShapeDtypeStruct((remote, rows, width), BF16)],
        flops=2 * remote * rows * in_width * (rows + width),
    )[0]

    grad_scale = (kernels / (pair_count * columns * planes * rows)) ** 0.5

    def exchange(deep):
        slots = planes * deep
        place = plane_of * deep + rank
        codes = code.reshape(planes, depth)[:, :deep].reshape(slots)
        boxes = [jax.ShapeDtypeStruct((slots, rows, width), BF16)]

        packed = call(pack_kernel, (jnp.maximum(codes, 0),), (column_cot,), boxes)[0]
        upstream = axis_exchange(packed, PLANE)

        resident, in_sum, w_sum = call(
            local_kernel,
            (pair_offset[:local], pair_block[:local], pair_dest_block[:local]),
            (after(picks[:local], packed), feats, feats_t, kern, cot_blocks),
            [jax.ShapeDtypeStruct((blocks, rows, width), F32)] + sums,
            flops=4 * local * rows * in_width * (rows + width),
        )
        placed = call(place_kernel, (place,), (after(parts, packed),), boxes)[0]
        came = axis_exchange(after(placed, upstream, resident), PLANE)

        in_sum, w_sum = call(
            remote_kernel,
            (pair_offset[local:], pair_block[local:], place),
            (picks[local:], feats_t, kern, upstream, in_sum, w_sum),
            sums,
            flops=2 * remote * rows * in_width * (rows + width),
        )
        in_sum = in_sum.reshape(row_count, in_width)
        mine = lax.dynamic_slice_in_dim(in_sum, chan * width, width, 1)
        theirs = lax.dynamic_slice_in_dim(in_sum, (1 - chan) * width, width, 1)
        theirs = lax.ppermute(theirs.astype(BF16), "chan", [(0, 1), (1, 0)])
        input_grad = (mine + theirs.astype(F32)).astype(BF16)

        flat = w_sum.reshape(kernels * in_width, width).astype(BF16)
        pieces = axis_exchange(after(flat, came), PLANE)
        column_sum = call(
            column_kernel,
            (after(jnp.where(codes < 0, columns * blocks, codes), flat, in_sum),),
            (came,),
            [jax.ShapeDtypeStruct((columns * blocks, rows, width), BF16)],
            [pltpu.VMEM((columns * blocks + 1, rows, width), F32)],
        )[0]
        arrived = lax.psum_scatter(column_sum, "z", scatter_dimension=0, tiled=True)
        whole = spread_weights(after(pieces, column_sum), planes, columns)
        weight_grad = (whole.astype(F32) * grad_scale).reshape(kernels, in_width, width)
        output = (resident + arrived.astype(F32)).reshape(row_count, width).astype(BF16)
        return output, input_grad, weight_grad

    return lax.switch(tier, [functools.partial(exchange, deep) for deep in depths])


def solution(mesh):
    x, y, z = FACTORS[mesh.devices.shape[0]]
    split = Mesh(mesh.devices.reshape(x, y, z, -1), SPACE + ("chan",))
    in_specs = (
        P(SPACE, "chan"),
        P(),
        P(SPACE, "chan"),
        P(SPACE),
        P(SPACE),
        P(SPACE, None),
        P(SPACE, None),
        P(SPACE),
        P(SPACE, None),
    )
    out_specs = (P(SPACE, "chan"), P(SPACE, "chan"), P(None, None, "chan"))
    return jax.shard_map(body, mesh=split, in_specs=in_specs, out_specs=out_specs, check_vma=False)
```

```python
import functools

import jax
import jax.numpy as jnp
from jax import lax
from jax.experimental import pallas as pl
from jax.experimental.pallas import tpu as pltpu
from jax.sharding import Mesh
from jax.sharding import PartitionSpec as P

SPACE = ("x", "y", "z")
PLANE = ("x", "y")
SHARES = (11, 13, 16)
FACTORS = {128: (4, 4, 8), 8: (2, 2, 2)}
BF16 = jnp.bfloat16
F32 = jnp.float32

VM = pl.BlockSpec(memory_space=pltpu.VMEM)
SM = pl.BlockSpec(memory_space=pltpu.SMEM)


def pick_transposed(rows_ref, at, block_rows):
    rows = rows_ref[pl.ds(at, 1), :]
    lines = lax.broadcasted_iota(jnp.int32, (block_rows, rows.shape[1]), 0)
    return jnp.where(lines == rows, 1.0, 0.0).astype(BF16)


def forward_block(picked, feats, kernel):
    rows = lax.dot_general(
        picked, feats, (((0,), (0,)), ((), ())), preferred_element_type=F32
    ).astype(BF16)
    return jnp.dot(rows, kernel, preferred_element_type=F32)


def backward_block(picked, upstream, feats_t, kernel, in_ref, block, w_ref, offset):
    spread = jnp.dot(picked, upstream, preferred_element_type=F32).astype(BF16)
    in_ref[block] += lax.dot_general(
        spread, kernel, (((1,), (1,)), ((), ())), preferred_element_type=F32
    )
    w_ref[offset] += jnp.dot(feats_t, spread, preferred_element_type=F32)


def send_kernel(offset, block, rows_ref, feat_ref, kern_ref, out_ref):
    def step(q, carry):
        picked = pick_transposed(rows_ref, q, feat_ref.shape[1])
        out_ref[q] = forward_block(picked, feat_ref[block[q]], kern_ref[offset[q]]).astype(BF16)
        return carry

    lax.fori_loop(0, rows_ref.shape[0], step, 0, unroll=4)


def place_kernel(slot, part_ref, out_ref):
    def step(q, carry):
        out_ref[slot[q]] = part_ref[q]
        return carry

    lax.fori_loop(0, part_ref.shape[0], step, 0, unroll=8)


def pack_kernel(code, cot_ref, out_ref):
    def step(s, carry):
        out_ref[s] = cot_ref[code[s]]
        return carry

    lax.fori_loop(0, out_ref.shape[0], step, 0, unroll=8)


def local_kernel(
    offset, block, dest, rows_ref, feat_ref, feat_t_ref, kern_ref, cot_ref, res_ref, in_ref, w_ref
):
    res_ref[...] = jnp.zeros_like(res_ref)
    in_ref[...] = jnp.zeros_like(in_ref)
    w_ref[...] = jnp.zeros_like(w_ref)

    def step(q, carry):
        b, k, d = block[q], offset[q], dest[q]
        picked = pick_transposed(rows_ref, q, feat_ref.shape[1])
        kernel = kern_ref[k]
        res_ref[d] += forward_block(picked, feat_ref[b], kernel)
        backward_block(picked, cot_ref[d], feat_t_ref[b], kernel, in_ref, b, w_ref, k)
        return carry

    lax.fori_loop(0, rows_ref.shape[0], step, 0)


def remote_kernel(
    offset, block, slot, rows_ref, feat_t_ref, kern_ref, up_ref, in0_ref, w0_ref, in_ref, w_ref
):
    in_ref[...] = in0_ref[...]
    w_ref[...] = w0_ref[...]

    def step(q, carry):
        b, k = block[q], offset[q]
        picked = pick_transposed(rows_ref, q, feat_t_ref.shape[2])
        backward_block(
            picked, up_ref[slot[q]], feat_t_ref[b], kern_ref[k], in_ref, b, w_ref, k
        )
        return carry

    lax.fori_loop(0, rows_ref.shape[0], step, 0, unroll=2)


def column_kernel(code, recv_ref, out_ref, acc_ref):
    acc_ref[...] = jnp.zeros_like(acc_ref)

    def step(s, carry):
        acc_ref[code[s]] += recv_ref[s].astype(F32)
        return carry

    lax.fori_loop(0, recv_ref.shape[0], step, 0, unroll=4)

    def put(b, carry):
        out_ref[b] = acc_ref[b].astype(BF16)
        return carry

    lax.fori_loop(0, out_ref.shape[0], put, 0, unroll=8)


def call(kernel, scalars, arrays, outs, scratch=(), flops=0):
    moved = sum(a.size * a.dtype.itemsize for a in arrays)
    moved += sum(o.size * o.dtype.itemsize for o in outs)
    return pl.pallas_call(
        kernel,
        out_shape=outs,
        in_specs=[SM] * len(scalars) + [VM] * len(arrays),
        out_specs=[VM] * len(outs),
        scratch_shapes=list(scratch),
        cost_estimate=pl.CostEstimate(flops=flops, bytes_accessed=moved, transcendentals=0),
    )(*scalars, *arrays)


def after(a, *others):
    return lax.optimization_barrier((a,) + others)[0]


def axis_exchange(a, axes):
    return lax.all_to_all(a, axes, split_axis=0, concat_axis=0, tiled=True)


def spread(part, axes, count):
    copies = jnp.broadcast_to(part[None], (count,) + part.shape)
    return axis_exchange(copies.reshape((-1,) + part.shape[1:]), axes)


def summed(pieces, count):
    pieces = pieces.reshape((count, -1, pieces.shape[-1]))
    return jnp.sum(pieces.astype(F32), axis=0).astype(BF16)


def spread_weights(pieces, planes, columns):
    part = summed(pieces, planes)
    rows = part.shape[0]
    each = -(-rows // (columns * 16)) * 16
    part = jnp.pad(part, ((0, columns * each - rows), (0, 0)))
    part = summed(axis_exchange(part, "z"), columns)
    return spread(spread(part, "z", columns)[:rows], PLANE, planes)


def body(
    features,
    weights,
    cotangent,
    pair_offset,
    pair_block,
    pair_rows,
    pair_mask,
    pair_dest_block,
    remote_dest,
):
    columns = lax.axis_size("z")
    planes = lax.axis_size("x") * lax.axis_size("y")
    chan = lax.axis_index("chan")
    row_count, width = features.shape
    kernels, in_width, _ = weights.shape
    pair_count, rows = pair_rows.shape
    remote = remote_dest.shape[0]
    local = pair_count - remote
    blocks = row_count // rows
    depth = 2 * columns
    depths = sorted({depth * share // 16 for share in SHARES})

    column_cot = lax.all_gather(cotangent, "z", axis=0, tiled=True)
    column_cot = column_cot.reshape(columns * blocks, rows, width)

    dest = remote_dest[:, 0]
    plane_of = dest // columns
    wanted = (dest % columns) * blocks + pair_dest_block[local:]
    order = jnp.arange(remote, dtype=jnp.int32)
    same = (plane_of[:, None] == plane_of[None, :]) & (order[None, :] < order[:, None])
    rank = jnp.sum(same.astype(jnp.int32), axis=1)
    slot = plane_of * depth + rank
    hits = slot[None, :] == jnp.arange(planes * depth, dtype=jnp.int32)[:, None]
    sent_code = jnp.max(jnp.where(hits, wanted[None, :], -1), axis=1)
    sent_code = jnp.concatenate(
        [sent_code.reshape(planes, depth), jnp.broadcast_to(jnp.max(rank), (planes, 1))], axis=1
    )
    code = axis_exchange(sent_code.reshape(-1), PLANE).reshape(planes, depth + 1)
    most = spread(jnp.max(code[:, depth], keepdims=True), "z", columns)
    code = code[:, :depth]

    picks = jnp.where(pair_mask > 0, pair_rows, rows)
    kern = jnp.where(chan == 0, weights[:, :, :width], weights[:, :, width:])
    other = lax.ppermute(features, "chan", [(0, 1), (1, 0)])
    low = jnp.where(chan == 0, features, other)
    high = jnp.where(chan == 0, other, features)
    feats = jnp.concatenate([low, high], axis=1).reshape(blocks, rows, in_width)
    feats_t = jnp.swapaxes(feats, 1, 2)
    cot_blocks = cotangent.reshape(blocks, rows, width)
    sums = [
        jax.ShapeDtypeStruct((blocks, rows, in_width), F32),
        jax.ShapeDtypeStruct((kernels, in_width, width), F32),
    ]

    parts = call(
        send_kernel,
        (pair_offset[local:], pair_block[local:]),
        (picks[local:], feats, kern),
        [jax.ShapeDtypeStruct((remote, rows, width), BF16)],
        flops=2 * remote * rows * in_width * (rows + width),
    )[0]

    most = jnp.max(after(most, parts))
    tier = jnp.sum((most >= jnp.array(depths[:-1])).astype(jnp.int32))
    grad_scale = (kernels / (pair_count * columns * planes * rows)) ** 0.5

    def exchange(deep):
        slots = planes * deep
        place = plane_of * deep + rank
        codes = code[:, :deep].reshape(slots)
        boxes = [jax.ShapeDtypeStruct((slots, rows, width), BF16)]

        packed = call(pack_kernel, (jnp.maximum(codes, 0),), (column_cot,), boxes)[0]
        upstream = axis_exchange(packed, PLANE)

        resident, in_sum, w_sum = call(
            local_kernel,
            (pair_offset[:local], pair_block[:local], pair_dest_block[:local]),
            (after(picks[:local], packed), feats, feats_t, kern, cot_blocks),
            [jax.ShapeDtypeStruct((blocks, rows, width), F32)] + sums,
            flops=4 * local * rows * in_width * (rows + width),
        )
        placed = call(place_kernel, (place,), (after(parts, packed),), boxes)[0]
        came = axis_exchange(after(placed, upstream, resident), PLANE)

        in_sum, w_sum = call(
            remote_kernel,
            (pair_offset[local:], pair_block[local:], place),
            (picks[local:], feats_t, kern, upstream, in_sum, w_sum),
            sums,
            flops=2 * remote * rows * in_width * (rows + width),
        )
        in_sum = in_sum.reshape(row_count, in_width)
        mine = lax.dynamic_slice_in_dim(in_sum, chan * width, width, 1)
        theirs = lax.dynamic_slice_in_dim(in_sum, (1 - chan) * width, width, 1)
        theirs = lax.ppermute(theirs.astype(BF16), "chan", [(0, 1), (1, 0)])
        input_grad = (mine + theirs.astype(F32)).astype(BF16)

        flat = w_sum.reshape(kernels * in_width, width).astype(BF16)
        pieces = axis_exchange(after(flat, came), PLANE)
        column_sum = call(
            column_kernel,
            (after(jnp.where(codes < 0, columns * blocks, codes), flat, in_sum),),
            (came,),
            [jax.ShapeDtypeStruct((columns * blocks, rows, width), BF16)],
            [pltpu.VMEM((columns * blocks + 1, rows, width), F32)],
        )[0]
        arrived = lax.psum_scatter(column_sum, "z", scatter_dimension=0, tiled=True)
        whole = spread_weights(after(pieces, column_sum), planes, columns)
        weight_grad = (whole.astype(F32) * grad_scale).reshape(kernels, in_width, width)
        output = (resident + arrived.astype(F32)).reshape(row_count, width).astype(BF16)
        return output, input_grad, weight_grad

    return lax.switch(tier, [functools.partial(exchange, deep) for deep in depths])


def solution(mesh):
    x, y, z = FACTORS[mesh.devices.shape[0]]
    split = Mesh(mesh.devices.reshape(x, y, z, -1), SPACE + ("chan",))
    in_specs = (
        P(SPACE, "chan"),
        P(),
        P(SPACE, "chan"),
        P(SPACE),
        P(SPACE),
        P(SPACE, None),
        P(SPACE, None),
        P(SPACE),
        P(SPACE, None),
    )
    out_specs = (P(SPACE, "chan"), P(SPACE, "chan"), P(None, None, "chan"))
    return jax.shard_map(body, mesh=split, in_specs=in_specs, out_specs=out_specs, check_vma=False)
```

```python
import functools

import jax
import jax.numpy as jnp
from jax import lax
from jax.experimental import pallas as pl
from jax.experimental.pallas import tpu as pltpu
from jax.sharding import Mesh
from jax.sharding import PartitionSpec as P

SPACE = ("x", "y", "z")
PLANE = ("x", "y")
SHARES = (11, 13, 16)
FACTORS = {128: (4, 4, 8), 8: (2, 2, 2)}
BF16 = jnp.bfloat16
F32 = jnp.float32

VM = pl.BlockSpec(memory_space=pltpu.VMEM)
SM = pl.BlockSpec(memory_space=pltpu.SMEM)


def pick_transposed(rows_ref, at, block_rows):
    rows = rows_ref[pl.ds(at, 1), :]
    lines = lax.broadcasted_iota(jnp.int32, (block_rows, rows.shape[1]), 0)
    return jnp.where(lines == rows, 1.0, 0.0).astype(BF16)


def forward_block(picked, feats, kernel):
    rows = lax.dot_general(
        picked, feats, (((0,), (0,)), ((), ())), preferred_element_type=F32
    ).astype(BF16)
    return jnp.dot(rows, kernel, preferred_element_type=F32)


def backward_block(picked, upstream, feats_t, kernel, in_ref, block, w_ref, offset):
    spread = jnp.dot(picked, upstream, preferred_element_type=F32).astype(BF16)
    in_ref[block] += lax.dot_general(
        spread, kernel, (((1,), (1,)), ((), ())), preferred_element_type=F32
    )
    w_ref[offset] += jnp.dot(feats_t, spread, preferred_element_type=F32)


def send_kernel(offset, block, rows_ref, feat_ref, kern_ref, out_ref):
    def step(q, carry):
        picked = pick_transposed(rows_ref, q, feat_ref.shape[1])
        out_ref[q] = forward_block(picked, feat_ref[block[q]], kern_ref[offset[q]]).astype(BF16)
        return carry

    lax.fori_loop(0, rows_ref.shape[0], step, 0, unroll=4)


def place_kernel(slot, part_ref, out_ref):
    def step(q, carry):
        out_ref[slot[q]] = part_ref[q]
        return carry

    lax.fori_loop(0, part_ref.shape[0], step, 0, unroll=8)


def pack_kernel(code, cot_ref, out_ref):
    def step(s, carry):
        out_ref[s] = cot_ref[code[s]]
        return carry

    lax.fori_loop(0, out_ref.shape[0], step, 0, unroll=8)


def local_kernel(
    offset, block, dest, rows_ref, feat_ref, feat_t_ref, kern_ref, cot_ref, res_ref, in_ref, w_ref
):
    res_ref[...] = jnp.zeros_like(res_ref)
    in_ref[...] = jnp.zeros_like(in_ref)
    w_ref[...] = jnp.zeros_like(w_ref)

    def step(q, carry):
        b, k, d = block[q], offset[q], dest[q]
        picked = pick_transposed(rows_ref, q, feat_ref.shape[1])
        kernel = kern_ref[k]
        res_ref[d] += forward_block(picked, feat_ref[b], kernel)
        backward_block(picked, cot_ref[d], feat_t_ref[b], kernel, in_ref, b, w_ref, k)
        return carry

    lax.fori_loop(0, rows_ref.shape[0], step, 0, unroll=2)


def remote_kernel(
    offset, block, slot, rows_ref, feat_t_ref, kern_ref, up_ref, in0_ref, w0_ref, in_ref, w_ref
):
    in_ref[...] = in0_ref[...]
    w_ref[...] = w0_ref[...]

    def step(q, carry):
        b, k = block[q], offset[q]
        picked = pick_transposed(rows_ref, q, feat_t_ref.shape[2])
        backward_block(
            picked, up_ref[slot[q]], feat_t_ref[b], kern_ref[k], in_ref, b, w_ref, k
        )
        return carry

    lax.fori_loop(0, rows_ref.shape[0], step, 0, unroll=4)


def column_kernel(code, recv_ref, out_ref, acc_ref):
    acc_ref[...] = jnp.zeros_like(acc_ref)

    def step(s, carry):
        acc_ref[code[s]] += recv_ref[s].astype(F32)
        return carry

    lax.fori_loop(0, recv_ref.shape[0], step, 0, unroll=4)

    def put(b, carry):
        out_ref[b] = acc_ref[b].astype(BF16)
        return carry

    lax.fori_loop(0, out_ref.shape[0], put, 0, unroll=8)


def call(kernel, scalars, arrays, outs, scratch=(), flops=0):
    moved = sum(a.size * a.dtype.itemsize for a in arrays)
    moved += sum(o.size * o.dtype.itemsize for o in outs)
    return pl.pallas_call(
        kernel,
        out_shape=outs,
        in_specs=[SM] * len(scalars) + [VM] * len(arrays),
        out_specs=[VM] * len(outs),
        scratch_shapes=list(scratch),
        cost_estimate=pl.CostEstimate(flops=flops, bytes_accessed=moved, transcendentals=0),
    )(*scalars, *arrays)


def after(a, *others):
    return lax.optimization_barrier((a,) + others)[0]


def axis_exchange(a, axes):
    return lax.all_to_all(a, axes, split_axis=0, concat_axis=0, tiled=True)


def spread(part, axes, count):
    copies = jnp.broadcast_to(part[None], (count,) + part.shape)
    return axis_exchange(copies.reshape((-1,) + part.shape[1:]), axes)


def summed(pieces, count):
    pieces = pieces.reshape((count, -1, pieces.shape[-1]))
    return jnp.sum(pieces.astype(F32), axis=0).astype(BF16)


def spread_weights(pieces, planes, columns):
    part = summed(pieces, planes)
    rows = part.shape[0]
    each = -(-rows // (columns * 16)) * 16
    part = jnp.pad(part, ((0, columns * each - rows), (0, 0)))
    part = summed(axis_exchange(part, "z"), columns)
    return spread(spread(part, "z", columns)[:rows], PLANE, planes)


def body(
    features,
    weights,
    cotangent,
    pair_offset,
    pair_block,
    pair_rows,
    pair_mask,
    pair_dest_block,
    remote_dest,
):
    columns = lax.axis_size("z")
    planes = lax.axis_size("x") * lax.axis_size("y")
    chan = lax.axis_index("chan")
    row_count, width = features.shape
    kernels, in_width, _ = weights.shape
    pair_count, rows = pair_rows.shape
    remote = remote_dest.shape[0]
    local = pair_count - remote
    blocks = row_count // rows
    depth = 2 * columns
    depths = sorted({depth * share // 16 for share in SHARES})

    column_cot = lax.all_gather(cotangent, "z", axis=0, tiled=True)
    column_cot = column_cot.reshape(columns * blocks, rows, width)

    dest = remote_dest[:, 0]
    plane_of = dest // columns
    wanted = (dest % columns) * blocks + pair_dest_block[local:]
    order = jnp.arange(remote, dtype=jnp.int32)
    same = (plane_of[:, None] == plane_of[None, :]) & (order[None, :] < order[:, None])
    rank = jnp.sum(same.astype(jnp.int32), axis=1)
    slot = plane_of * depth + rank
    hits = slot[None, :] == jnp.arange(planes * depth, dtype=jnp.int32)[:, None]
    sent_code = jnp.max(jnp.where(hits, wanted[None, :], -1), axis=1)
    sent_code = jnp.concatenate(
        [sent_code.reshape(planes, depth), jnp.broadcast_to(jnp.max(rank), (planes, 1))], axis=1
    )
    code = axis_exchange(sent_code.reshape(-1), PLANE).reshape(planes, depth + 1)
    most = spread(jnp.max(code[:, depth], keepdims=True), "z", columns)
    code = code[:, :depth]

    picks = jnp.where(pair_mask > 0, pair_rows, rows)
    kern = jnp.where(chan == 0, weights[:, :, :width], weights[:, :, width:])
    other = lax.ppermute(features, "chan", [(0, 1), (1, 0)])
    low = jnp.where(chan == 0, features, other)
    high = jnp.where(chan == 0, other, features)
    feats = jnp.concatenate([low, high], axis=1).reshape(blocks, rows, in_width)
    feats_t = jnp.swapaxes(feats, 1, 2)
    cot_blocks = cotangent.reshape(blocks, rows, width)
    sums = [
        jax.ShapeDtypeStruct((blocks, rows, in_width), F32),
        jax.ShapeDtypeStruct((kernels, in_width, width), F32),
    ]

    parts = call(
        send_kernel,
        (pair_offset[local:], pair_block[local:]),
        (picks[local:], feats, kern),
        [jax.ShapeDtypeStruct((remote, rows, width), BF16)],
        flops=2 * remote * rows * in_width * (rows + width),
    )[0]

    most = jnp.max(after(most, parts))
    tier = jnp.sum((most >= jnp.array(depths[:-1])).astype(jnp.int32))
    grad_scale = (kernels / (pair_count * columns * planes * rows)) ** 0.5

    def exchange(deep):
        slots = planes * deep
        place = plane_of * deep + rank
        codes = code[:, :deep].reshape(slots)
        boxes = [jax.ShapeDtypeStruct((slots, rows, width), BF16)]

        packed = call(pack_kernel, (jnp.maximum(codes, 0),), (column_cot,), boxes)[0]
        upstream = axis_exchange(packed, PLANE)

        resident, in_sum, w_sum = call(
            local_kernel,
            (pair_offset[:local], pair_block[:local], pair_dest_block[:local]),
            (after(picks[:local], upstream), feats, feats_t, kern, cot_blocks),
            [jax.ShapeDtypeStruct((blocks, rows, width), F32)] + sums,
            flops=4 * local * rows * in_width * (rows + width),
        )
        placed = call(place_kernel, (place,), (after(parts, packed),), boxes)[0]
        came = axis_exchange(after(placed, upstream), PLANE)

        in_sum, w_sum = call(
            remote_kernel,
            (pair_offset[local:], pair_block[local:], place),
            (picks[local:], feats_t, kern, upstream, in_sum, w_sum),
            sums,
            flops=2 * remote * rows * in_width * (rows + width),
        )
        in_sum = in_sum.reshape(row_count, in_width)
        mine = lax.dynamic_slice_in_dim(in_sum, chan * width, width, 1)
        theirs = lax.dynamic_slice_in_dim(in_sum, (1 - chan) * width, width, 1)
        theirs = lax.ppermute(theirs.astype(BF16), "chan", [(0, 1), (1, 0)])
        input_grad = (mine + theirs.astype(F32)).astype(BF16)

        flat = w_sum.reshape(kernels * in_width, width).astype(BF16)
        pieces = axis_exchange(after(flat, came), PLANE)
        column_sum = call(
            column_kernel,
            (after(jnp.where(codes < 0, columns * blocks, codes), flat, in_sum),),
            (came,),
            [jax.ShapeDtypeStruct((columns * blocks, rows, width), BF16)],
            [pltpu.VMEM((columns * blocks + 1, rows, width), F32)],
        )[0]
        arrived = lax.psum_scatter(column_sum, "z", scatter_dimension=0, tiled=True)
        whole = spread_weights(after(pieces, column_sum), planes, columns)
        weight_grad = (whole.astype(F32) * grad_scale).reshape(kernels, in_width, width)
        output = (resident + arrived.astype(F32)).reshape(row_count, width).astype(BF16)
        return output, input_grad, weight_grad

    return lax.switch(tier, [functools.partial(exchange, deep) for deep in depths])


def solution(mesh):
    x, y, z = FACTORS[mesh.devices.shape[0]]
    split = Mesh(mesh.devices.reshape(x, y, z, -1), SPACE + ("chan",))
    in_specs = (
        P(SPACE, "chan"),
        P(),
        P(SPACE, "chan"),
        P(SPACE),
        P(SPACE),
        P(SPACE, None),
        P(SPACE, None),
        P(SPACE),
        P(SPACE, None),
    )
    out_specs = (P(SPACE, "chan"), P(SPACE, "chan"), P(None, None, "chan"))
    return jax.shard_map(body, mesh=split, in_specs=in_specs, out_specs=out_specs, check_vma=False)
```

```python
import functools

import jax
import jax.numpy as jnp
from jax import lax
from jax.experimental import pallas as pl
from jax.experimental.pallas import tpu as pltpu
from jax.sharding import Mesh
from jax.sharding import PartitionSpec as P

SPACE = ("x", "y", "z")
PLANE = ("x", "y")
SHARES = (11, 13, 16)
FACTORS = {128: (4, 4, 8), 8: (2, 2, 2)}
BF16 = jnp.bfloat16
F32 = jnp.float32

VM = pl.BlockSpec(memory_space=pltpu.VMEM)
SM = pl.BlockSpec(memory_space=pltpu.SMEM)


def pick_transposed(rows_ref, at, block_rows):
    rows = rows_ref[pl.ds(at, 1), :]
    lines = lax.broadcasted_iota(jnp.int32, (block_rows, rows.shape[1]), 0)
    return jnp.where(lines == rows, 1.0, 0.0).astype(BF16)


def forward_block(picked, feats, kernel):
    rows = lax.dot_general(
        picked, feats, (((0,), (0,)), ((), ())), preferred_element_type=F32
    ).astype(BF16)
    return jnp.dot(rows, kernel, preferred_element_type=F32)


def backward_block(picked, upstream, feats_t, kernel, in_ref, block, w_ref, offset):
    spread = jnp.dot(picked, upstream, preferred_element_type=F32).astype(BF16)
    in_ref[block] += lax.dot_general(
        spread, kernel, (((1,), (1,)), ((), ())), preferred_element_type=F32
    )
    w_ref[offset] += jnp.dot(feats_t, spread, preferred_element_type=F32)


def send_kernel(offset, block, rows_ref, feat_ref, kern_ref, out_ref):
    def step(q, carry):
        picked = pick_transposed(rows_ref, q, feat_ref.shape[1])
        out_ref[q] = forward_block(picked, feat_ref[block[q]], kern_ref[offset[q]]).astype(BF16)
        return carry

    lax.fori_loop(0, rows_ref.shape[0], step, 0, unroll=4)


def place_kernel(slot, part_ref, out_ref):
    def step(q, carry):
        out_ref[slot[q]] = part_ref[q]
        return carry

    lax.fori_loop(0, part_ref.shape[0], step, 0, unroll=8)


def pack_kernel(first, code, cot_ref, out_ref):
    def step(s, carry):
        out_ref[s] = cot_ref[code[s], first : first + out_ref.shape[1]]
        return carry

    lax.fori_loop(0, out_ref.shape[0], step, 0, unroll=8)


def local_kernel(
    offset, block, dest, rows_ref, feat_ref, feat_t_ref, kern_ref, cot_ref, res_ref, in_ref, w_ref
):
    res_ref[...] = jnp.zeros_like(res_ref)
    in_ref[...] = jnp.zeros_like(in_ref)
    w_ref[...] = jnp.zeros_like(w_ref)

    def step(q, carry):
        b, k, d = block[q], offset[q], dest[q]
        picked = pick_transposed(rows_ref, q, feat_ref.shape[1])
        kernel = kern_ref[k]
        res_ref[d] += forward_block(picked, feat_ref[b], kernel)
        backward_block(picked, cot_ref[d], feat_t_ref[b], kernel, in_ref, b, w_ref, k)
        return carry

    lax.fori_loop(0, rows_ref.shape[0], step, 0, unroll=2)


def remote_kernel(
    offset, block, slot, rows_ref, feat_t_ref, kern_ref, top_ref, low_ref, in0_ref, w0_ref, in_ref, w_ref
):
    in_ref[...] = in0_ref[...]
    w_ref[...] = w0_ref[...]

    def step(q, carry):
        b, k = block[q], offset[q]
        picked = pick_transposed(rows_ref, q, feat_t_ref.shape[2])
        upstream = jnp.concatenate([top_ref[slot[q]], low_ref[slot[q]]], axis=0)
        backward_block(picked, upstream, feat_t_ref[b], kern_ref[k], in_ref, b, w_ref, k)
        return carry

    lax.fori_loop(0, rows_ref.shape[0], step, 0, unroll=4)


def column_kernel(code, recv_ref, out_ref, acc_ref):
    acc_ref[...] = jnp.zeros_like(acc_ref)

    def step(s, carry):
        acc_ref[code[s]] += recv_ref[s].astype(F32)
        return carry

    lax.fori_loop(0, recv_ref.shape[0], step, 0, unroll=4)

    def put(b, carry):
        out_ref[b] = acc_ref[b].astype(BF16)
        return carry

    lax.fori_loop(0, out_ref.shape[0], put, 0, unroll=8)


def call(kernel, scalars, arrays, outs, scratch=(), flops=0):
    moved = sum(a.size * a.dtype.itemsize for a in arrays)
    moved += sum(o.size * o.dtype.itemsize for o in outs)
    return pl.pallas_call(
        kernel,
        out_shape=outs,
        in_specs=[SM] * len(scalars) + [VM] * len(arrays),
        out_specs=[VM] * len(outs),
        scratch_shapes=list(scratch),
        cost_estimate=pl.CostEstimate(flops=flops, bytes_accessed=moved, transcendentals=0),
    )(*scalars, *arrays)


def after(a, *others):
    return lax.optimization_barrier((a,) + others)[0]


def axis_exchange(a, axes):
    return lax.all_to_all(a, axes, split_axis=0, concat_axis=0, tiled=True)


def spread(part, axes, count):
    copies = jnp.broadcast_to(part[None], (count,) + part.shape)
    return axis_exchange(copies.reshape((-1,) + part.shape[1:]), axes)


def summed(pieces, count):
    pieces = pieces.reshape((count, -1, pieces.shape[-1]))
    return jnp.sum(pieces.astype(F32), axis=0).astype(BF16)


def spread_weights(pieces, planes, columns):
    part = summed(pieces, planes)
    rows = part.shape[0]
    each = -(-rows // (columns * 16)) * 16
    part = jnp.pad(part, ((0, columns * each - rows), (0, 0)))
    part = summed(axis_exchange(part, "z"), columns)
    return spread(spread(part, "z", columns)[:rows], PLANE, planes)


def body(
    features,
    weights,
    cotangent,
    pair_offset,
    pair_block,
    pair_rows,
    pair_mask,
    pair_dest_block,
    remote_dest,
):
    columns = lax.axis_size("z")
    planes = lax.axis_size("x") * lax.axis_size("y")
    chan = lax.axis_index("chan")
    row_count, width = features.shape
    kernels, in_width, _ = weights.shape
    pair_count, rows = pair_rows.shape
    remote = remote_dest.shape[0]
    local = pair_count - remote
    blocks = row_count // rows
    depth = 2 * columns
    depths = sorted({depth * share // 16 for share in SHARES})

    column_cot = lax.all_gather(cotangent, "z", axis=0, tiled=True)
    column_cot = column_cot.reshape(columns * blocks, rows, width)

    dest = remote_dest[:, 0]
    plane_of = dest // columns
    wanted = (dest % columns) * blocks + pair_dest_block[local:]
    order = jnp.arange(remote, dtype=jnp.int32)
    same = (plane_of[:, None] == plane_of[None, :]) & (order[None, :] < order[:, None])
    rank = jnp.sum(same.astype(jnp.int32), axis=1)
    slot = plane_of * depth + rank
    hits = slot[None, :] == jnp.arange(planes * depth, dtype=jnp.int32)[:, None]
    sent_code = jnp.max(jnp.where(hits, wanted[None, :], -1), axis=1)
    sent_code = jnp.concatenate(
        [sent_code.reshape(planes, depth), jnp.broadcast_to(jnp.max(rank), (planes, 1))], axis=1
    )
    code = axis_exchange(sent_code.reshape(-1), PLANE).reshape(planes, depth + 1)
    most = spread(jnp.max(code[:, depth], keepdims=True), "z", columns)
    code = code[:, :depth]

    picks = jnp.where(pair_mask > 0, pair_rows, rows)
    kern = jnp.where(chan == 0, weights[:, :, :width], weights[:, :, width:])
    other = lax.ppermute(features, "chan", [(0, 1), (1, 0)])
    low = jnp.where(chan == 0, features, other)
    high = jnp.where(chan == 0, other, features)
    feats = jnp.concatenate([low, high], axis=1).reshape(blocks, rows, in_width)
    feats_t = jnp.swapaxes(feats, 1, 2)
    cot_blocks = cotangent.reshape(blocks, rows, width)
    sums = [
        jax.ShapeDtypeStruct((blocks, rows, in_width), F32),
        jax.ShapeDtypeStruct((kernels, in_width, width), F32),
    ]

    parts = call(
        send_kernel,
        (pair_offset[local:], pair_block[local:]),
        (picks[local:], feats, kern),
        [jax.ShapeDtypeStruct((remote, rows, width), BF16)],
        flops=2 * remote * rows * in_width * (rows + width),
    )[0]

    most = jnp.max(after(most, parts))
    tier = jnp.sum((most >= jnp.array(depths[:-1])).astype(jnp.int32))
    grad_scale = (kernels / (pair_count * columns * planes * rows)) ** 0.5

    def exchange(deep):
        slots = planes * deep
        place = plane_of * deep + rank
        codes = code[:, :deep].reshape(slots)
        boxes = [jax.ShapeDtypeStruct((slots, rows, width), BF16)]

        half = rows // 2
        halves = [jax.ShapeDtypeStruct((slots, half, width), BF16)]
        asked = jnp.maximum(codes, 0)
        packed = call(functools.partial(pack_kernel, 0), (asked,), (column_cot,), halves)[0]
        top = axis_exchange(packed, PLANE)
        asked = after(asked, packed)
        lower = call(functools.partial(pack_kernel, half), (asked,), (column_cot,), halves)[0]
        low = axis_exchange(after(lower, top), PLANE)

        resident, in_sum, w_sum = call(
            local_kernel,
            (pair_offset[:local], pair_block[:local], pair_dest_block[:local]),
            (after(picks[:local], low), feats, feats_t, kern, cot_blocks),
            [jax.ShapeDtypeStruct((blocks, rows, width), F32)] + sums,
            flops=4 * local * rows * in_width * (rows + width),
        )
        placed = call(place_kernel, (place,), (after(parts, lower),), boxes)[0]
        came = axis_exchange(after(placed, low), PLANE)

        in_sum, w_sum = call(
            remote_kernel,
            (pair_offset[local:], pair_block[local:], place),
            (picks[local:], feats_t, kern, top, low, in_sum, w_sum),
            sums,
            flops=2 * remote * rows * in_width * (rows + width),
        )
        in_sum = in_sum.reshape(row_count, in_width)
        mine = lax.dynamic_slice_in_dim(in_sum, chan * width, width, 1)
        theirs = lax.dynamic_slice_in_dim(in_sum, (1 - chan) * width, width, 1)
        theirs = lax.ppermute(theirs.astype(BF16), "chan", [(0, 1), (1, 0)])
        input_grad = (mine + theirs.astype(F32)).astype(BF16)

        flat = w_sum.reshape(kernels * in_width, width).astype(BF16)
        pieces = axis_exchange(after(flat, came), PLANE)
        column_sum = call(
            column_kernel,
            (after(jnp.where(codes < 0, columns * blocks, codes), flat, in_sum),),
            (came,),
            [jax.ShapeDtypeStruct((columns * blocks, rows, width), BF16)],
            [pltpu.VMEM((columns * blocks + 1, rows, width), F32)],
        )[0]
        arrived = lax.psum_scatter(column_sum, "z", scatter_dimension=0, tiled=True)
        whole = spread_weights(after(pieces, column_sum), planes, columns)
        weight_grad = (whole.astype(F32) * grad_scale).reshape(kernels, in_width, width)
        output = (resident + arrived.astype(F32)).reshape(row_count, width).astype(BF16)
        return output, input_grad, weight_grad

    return lax.switch(tier, [functools.partial(exchange, deep) for deep in depths])


def solution(mesh):
    x, y, z = FACTORS[mesh.devices.shape[0]]
    split = Mesh(mesh.devices.reshape(x, y, z, -1), SPACE + ("chan",))
    in_specs = (
        P(SPACE, "chan"),
        P(),
        P(SPACE, "chan"),
        P(SPACE),
        P(SPACE),
        P(SPACE, None),
        P(SPACE, None),
        P(SPACE),
        P(SPACE, None),
    )
    out_specs = (P(SPACE, "chan"), P(SPACE, "chan"), P(None, None, "chan"))
    return jax.shard_map(body, mesh=split, in_specs=in_specs, out_specs=out_specs, check_vma=False)
```
